32 devices in a mesh: gx: 16 (over z, y, core), gy: 2 (over x).
Axes of the slice: x: 2, y: 2, z: 4, core: 2. Of those that a mesh axis runs over, the one named last changes fastest.
Arguments:
- displacement: float32 [3, 128, 32, 512], P(None, 'gx', 'gy'), may hold values from -1.2 to 1.2
- density: float32 [128, 32, 512], P('gx', 'gy'), may hold values from 0.1 to 1
- stiffness: float32 [24, 24], replicated, may hold values from -16 to 17, as said below
Outputs:
- sensitivity: float32 [128, 32, 512], P('gx', 'gy')
- filtered: float32 [128, 32, 512], P('gx', 'gy')
The draws below stay inside these ranges and needn't reach their ends.
Inputs may be any that keep to these rules, and one draw needn't show every extreme that they name: `stiffness`: symmetric positive definite.
All inputs are finite; a program needn't handle non-finite values.
Results may differ from the reference program's by a relative error of at most 0.00025.
Values sent between devices are 32-bit elements; how exact they have to be, the bound alone decides.
A program may use at most 64 MiB of HBM per device.

```python
import jax
import jax.numpy as jnp
from jax import lax

NZ = 512
DOFS = 24
ITERS = 3
NX = 128
NY = 32


def blend_weight(key):
    phases = jax.random.uniform(jax.random.fold_in(key, 7), (2,), jnp.float32, 0.0, 6.2831853)
    pos_x = (jnp.arange(NX).astype(jnp.float32) + 0.5) / NX
    pos_y = (jnp.arange(NY).astype(jnp.float32) + 0.5) / NY
    wave = 0.6 * jnp.sin(6.2831853 * 1.5 * pos_x[:, None] + phases[0]) + 0.4 * jnp.sin(6.2831853 * pos_y[None, :] + phases[1])
    return 0.5 + 0.5 * wave


def draw_displacement(key, part):
    weight = blend_weight(key)[None, :, :, None]
    position = jnp.arange(NX).astype(jnp.float32) / NX
    spread = (0.1 + 0.2 * position)[None, :, None, None]
    pos_x = (jnp.arange(NX).astype(jnp.float32) + 0.5) / NX
    pos_y = (jnp.arange(NY).astype(jnp.float32) + 0.5) / NY
    pos_z = (jnp.arange(NZ).astype(jnp.float32) + 0.5) / NZ
    phases = jax.random.uniform(jax.random.fold_in(key, 11), (3,), jnp.float32, 0.0, 6.2831853)
    argument = 0.7 * pos_x[:, None, None] + 0.5 * pos_y[None, :, None] + 0.3 * pos_z[None, None, :]
    smooth = 2.5 * jnp.sin(6.2831853 * argument[None] + phases[:, None, None, None])
    rough = jax.random.truncated_normal(key, -4.0, 4.0, (3, NX, NY, NZ), jnp.float32)
    return spread * ((1.0 - weight) * rough + weight * smooth)


def draw_density(key, part):
    weight = blend_weight(key)[:, :, None]
    lowest = 0.1 + 0.4 * weight
    unit = jax.random.uniform(jax.random.fold_in(key, 13), (NX, NY, NZ), jnp.float32)
    return lowest + (1.0 - lowest) * unit


def draw_stiffness(key, part):
    factor = jax.random.truncated_normal(key, -4.0, 4.0, (DOFS, DOFS), jnp.float32)
    product = jnp.dot(factor, factor.T, precision=jax.lax.Precision.HIGHEST) / DOFS
    return product + jnp.eye(DOFS, dtype=jnp.float32)


def setup_inputs(seed: int = 0) -> dict:
    key_list = jax.random.split(jax.random.key(seed), 4)
    displacement = draw_displacement(jax.random.fold_in(key_list[3], 71), 0)
    density = draw_density(jax.random.fold_in(key_list[3], 71), 0)
    stiffness = draw_stiffness(jax.random.fold_in(key_list[3], 71), 0)
    return {"displacement": displacement, "density": density, "stiffness": stiffness}


penal = 3.0
e_min = 0.001
filter_weight = 2.0


def corner_rows(block, size_x, size_y, size_z):
    rows = []
    for offset_x in (0, 1):
        for offset_y in (0, 1):
            for offset_z in (0, 1):
                for comp in range(3):
                    piece = block[comp, offset_x:offset_x + size_x, offset_y:offset_y + size_y, offset_z:offset_z + size_z]
                    rows.append(piece.reshape(-1))
    return jnp.stack(rows, axis=0)


def element_energy(stacked, stiffness):
    weighted = jnp.dot(stiffness, stacked, precision=lax.Precision.HIGHEST, preferred_element_type=jnp.float32)
    return jnp.sum(weighted * stacked, axis=0)


def neighbour_count():
    index_x = jnp.arange(NX)[:, None, None]
    index_y = jnp.arange(NY)[None, :, None]
    index_z = jnp.arange(NZ)[None, None, :]
    missing = (index_x == 0).astype(jnp.float32) + (index_x == NX - 1).astype(jnp.float32)
    missing = missing + (index_y == 0).astype(jnp.float32) + (index_y == NY - 1).astype(jnp.float32)
    missing = missing + (index_z == 0).astype(jnp.float32) + (index_z == NZ - 1).astype(jnp.float32)
    return 6.0 - missing


def apply_filter(field, neighbours):
    padded = jnp.pad(field, 1)
    beside = padded[2:, 1:-1, 1:-1] + padded[:-2, 1:-1, 1:-1]
    beside = beside + padded[1:-1, 2:, 1:-1] + padded[1:-1, :-2, 1:-1]
    beside = beside + padded[1:-1, 1:-1, 2:] + padded[1:-1, 1:-1, :-2]
    return (1.0 + filter_weight * neighbours) * field - filter_weight * beside


def reference(displacement, density, stiffness):
    padded = jnp.pad(displacement, ((0, 0), (0, 1), (0, 1), (0, 1)))

    def slab_energy(index):
        block = lax.dynamic_slice_in_dim(padded, index, 2, 1)
        stacked = corner_rows(block, 1, NY, NZ)
        return element_energy(stacked, stiffness).reshape(NY, NZ)

    energy = lax.map(slab_energy, jnp.arange(NX).astype(jnp.int32))
    sensitivity = -penal * density * density * (1.0 - e_min) * energy
    neighbours = neighbour_count()
    inverse = 1.0 / (1.0 + filter_weight * neighbours)
    solution = jnp.zeros_like(sensitivity)
    residual = sensitivity
    scaled = inverse * residual
    direction = scaled
    residual_dot = jnp.sum(residual * scaled)
    for iteration in range(ITERS):
        image = apply_filter(direction, neighbours)
        step_size = residual_dot / jnp.sum(direction * image)
        solution = solution + step_size * direction
        residual = residual - step_size * image
        scaled = inverse * residual
        next_dot = jnp.sum(residual * scaled)
        direction = scaled + (next_dot / residual_dot) * direction
        residual_dot = next_dot
    return sensitivity, solution
```

```python
import functools

import jax
import jax.numpy as jnp
from jax import lax
from jax.experimental import pallas as pl
from jax.experimental.pallas import tpu as pltpu
from jax.sharding import PartitionSpec as P

MESH = pl.DeviceIdType.MESH
penal = 3.0
e_min = 0.001
filter_weight = 2.0


def kernel(
    n_x, n_y,
    disp, dens, stiff,
    sens, filt,
    views, x_in, y_out, y_in, c_out, c_in,
    field0, field1, field2, image0, image1, image2, face_out, face_in, dots_out, dots_in,
    halo_send, halo_recv, face_send, face_recv, dots_send, dots_recv,
):
    size_x, size_y, size_z = dens.shape
    me_x, me_y = lax.axis_index("gx"), lax.axis_index("gy")
    me = me_x * n_y + me_y
    count = n_x * n_y
    has_xp, has_xn = me_x > 0, me_x < n_x - 1
    has_yp, has_yn = me_y > 0, me_y < n_y - 1

    def place(index):
        return {"gx": index // n_y, "gy": lax.rem(index, n_y)}

    barrier = pltpu.get_barrier_semaphore()

    @pl.loop(1, count)
    def _(offset):
        pl.semaphore_signal(
            barrier, inc=1, device_id=place(lax.rem(me + offset, count)), device_id_type=MESH
        )

    c_out[...] = jnp.zeros_like(c_out)
    for m in range(3):
        for i in range(size_x):
            y_out[m, i : i + 1, :] = disp[m, i, 0:1, :]
        c_out[m : m + 1, :] = disp[m, 0, 0:1, :]

    @pl.when(jnp.logical_not(has_xn))
    def _():
        x_in[...] = jnp.zeros_like(x_in)
        for field in (field0, field1, field2):
            field[size_x + 1] = jnp.zeros((size_y, size_z), jnp.float32)

    @pl.when(jnp.logical_not(has_xp))
    def _():
        for field in (field0, field1, field2):
            field[0] = jnp.zeros((size_y, size_z), jnp.float32)

    @pl.when(jnp.logical_not(has_yn))
    def _():
        y_in[...] = jnp.zeros_like(y_in)
        for step in range(3):
            face_in[step, 1] = jnp.zeros((size_x, size_z), jnp.float32)

    @pl.when(jnp.logical_not(has_yp))
    def _():
        for step in range(3):
            face_in[step, 0] = jnp.zeros((size_x, size_z), jnp.float32)

    @pl.when(jnp.logical_not(jnp.logical_and(has_xn, has_yn)))
    def _():
        c_in[...] = jnp.zeros_like(c_in)

    pl.semaphore_wait(barrier, count - 1)

    def remote(src, dst, send, recv, to_x, to_y):
        return pltpu.make_async_remote_copy(
            src_ref=src, dst_ref=dst, send_sem=send, recv_sem=recv,
            device_id={"gx": to_x, "gy": to_y}, device_id_type=MESH,
        )

    halo_x = remote(disp.at[:, 0], x_in, halo_send.at[0], halo_recv.at[0], me_x - 1, me_y)
    halo_y = remote(y_out, y_in, halo_send.at[1], halo_recv.at[1], me_x, me_y - 1)
    halo_c = remote(c_out, c_in, halo_send.at[2], halo_recv.at[2], me_x - 1, me_y - 1)
    halos = (
        (halo_x, has_xp, has_xn),
        (halo_y, has_yp, has_yn),
        (halo_c, jnp.logical_and(has_xp, has_yp), jnp.logical_and(has_xn, has_yn)),
    )
    for copy, sends, _ in halos:
        pl.when(sends)(copy.start)

    rows = lax.broadcasted_iota(jnp.int32, (size_y, size_z), 0)
    lanes = lax.broadcasted_iota(jnp.int32, (size_y, size_z), 1)

    def later_z(value):
        return jnp.where(lanes == size_z - 1, 0.0, pltpu.roll(value, size_z - 1, 1))

    def earlier_z(value):
        return jnp.where(lanes == 0, 0.0, pltpu.roll(value, 1, 1))

    def put_views(m, i, value, last_row):
        upper = pltpu.roll(value, size_y - 1, 0)
        if last_row is not None:
            upper = jnp.where(rows == size_y - 1, jnp.broadcast_to(last_row, value.shape), upper)
        views[0, m, i] = value
        views[1, m, i] = later_z(value)
        views[2, m, i] = upper
        views[3, m, i] = later_z(upper)

    @pl.loop(0, size_x)
    def _(i):
        for m in range(3):
            put_views(m, i, disp[m, i], None)

    def energy_block(i, start):
        def view(dof):
            a, b, c, m = dof // 12, dof // 6 % 2, dof // 3 % 2, dof % 3
            return views[2 * b + c, m, i + a, start : start + 8, :]

        energy = None
        for row in range(24):
            weighted = (0.5 * stiff[row, row]) * view(row)
            for col in range(row + 1, 24):
                weighted = weighted + stiff[row, col] * view(col)
            term = view(row) * weighted
            energy = term if energy is None else energy + term
        rho = dens[i, start : start + 8, :]
        sens[i, start : start + 8, :] = (-2.0 * penal * (1.0 - e_min)) * (rho * rho) * energy

    @pl.loop(0, size_x - 1)
    def _(i):
        energy_block(i, 0)

    for copy, sends, receives in halos:
        pl.when(receives)(copy.wait_recv)
    for m in range(3):
        put_views(m, size_x, x_in[m], c_in[m : m + 1, :])

    @pl.loop(0, size_x)
    def _(i):
        for m in range(3):
            last = y_in[m, pl.ds(i, 1), :]
            views[2, m, i, size_y - 1 : size_y, :] = last
            views[3, m, i, size_y - 1 : size_y, :] = jnp.where(
                lanes[:1] == size_z - 1, 0.0, pltpu.roll(last, size_z - 1, 1)
            )

    for start in range(8, size_y, 8):
        @pl.loop(0, size_x)
        def _(i):
            energy_block(i, start)

    energy_block(size_x - 1, 0)

    for copy, sends, _ in halos:
        pl.when(sends)(copy.wait_send)

    plane = 6.0 - (lanes == 0).astype(jnp.float32) - (lanes == size_z - 1).astype(jnp.float32)
    row_low = jnp.logical_and(rows == 0, jnp.logical_not(has_yp))
    row_high = jnp.logical_and(rows == size_y - 1, jnp.logical_not(has_yn))
    plane = plane - row_low.astype(jnp.float32) - row_high.astype(jnp.float32)

    def diagonal(i):
        at_low = jnp.logical_and(i == 0, jnp.logical_not(has_xp))
        at_high = jnp.logical_and(i == size_x - 1, jnp.logical_not(has_xn))
        missing = at_low.astype(jnp.float32) + at_high.astype(jnp.float32)
        return 1.0 + filter_weight * (plane - missing)

    def put_field(step, field, i, value):
        field[i + 1] = value
        face_out[step, 0, pl.ds(i, 1), :] = value[0:1]
        face_out[step, 1, pl.ds(i, 1), :] = value[size_y - 1 : size_y]

    def faces(step, field):
        return (
            (remote(field.at[1], field.at[size_x + 1], face_send.at[step, 0],
                    face_recv.at[step, 0], me_x - 1, me_y), has_xp, has_xn),
            (remote(field.at[size_x], field.at[0], face_send.at[step, 1],
                    face_recv.at[step, 1], me_x + 1, me_y), has_xn, has_xp),
            (remote(face_out.at[step, 0], face_in.at[step, 1], face_send.at[step, 2],
                    face_recv.at[step, 2], me_x, me_y - 1), has_yp, has_yn),
            (remote(face_out.at[step, 1], face_in.at[step, 0], face_send.at[step, 3],
                    face_recv.at[step, 3], me_x, me_y + 1), has_yn, has_yp),
        )

    def exchange(step, field):
        copies = faces(step, field)
        for copy, sends, _ in copies:
            pl.when(sends)(copy.start)
        for copy, _, receives in copies:
            pl.when(receives)(copy.wait_recv)
        return copies

    def apply(step, field, i):
        value = field[i + 1]
        below = jnp.where(rows == 0, jnp.broadcast_to(face_in[step, 0, pl.ds(i, 1), :], value.shape),
                          pltpu.roll(value, 1, 0))
        above = jnp.where(rows == size_y - 1,
                          jnp.broadcast_to(face_in[step, 1, pl.ds(i, 1), :], value.shape),
                          pltpu.roll(value, size_y - 1, 0))
        beside = field[i] + field[i + 2] + below + above + later_z(value) + earlier_z(value)
        return diagonal(i) * value - filter_weight * beside

    def fold(value):
        part = value[0:8]
        for start in range(8, size_y, 8):
            part = part + value[start : start + 8]
        total = part[:, 0:128]
        for start in range(128, size_z, 128):
            total = total + part[:, start : start + 128]
        return total

    tile_row = lax.broadcasted_iota(jnp.int32, (8, 128), 0)
    tile_lane = lax.broadcasted_iota(jnp.int32, (8, 128), 1)

    def send_dots(which, parts):
        packed = jnp.zeros((8, 128), jnp.float32)
        for index, part in enumerate(parts):
            packed = packed + jnp.where(
                tile_row == index, jnp.broadcast_to(jnp.sum(part, axis=0, keepdims=True), (8, 128)), 0.0
            )
        totals = jnp.broadcast_to(jnp.sum(packed, axis=1, keepdims=True), (8, 128))
        row = jnp.sum(jnp.where(tile_row == tile_lane, totals, 0.0), axis=0, keepdims=True)
        dots_out[which] = row
        dots_in[which, count - 1] = row

        @pl.loop(1, count)
        def _(offset):
            to = place(lax.rem(me + offset, count))
            remote(dots_out.at[which], dots_in.at[which, offset - 1], dots_send.at[which],
                   dots_recv.at[which], to["gx"], to["gy"]).start()

    def take_dots(which, number):
        whole = dots_in.at[which, pl.ds(0, count - 1)]
        pltpu.make_async_copy(whole, whole, dots_recv.at[which]).wait()
        row = jnp.sum(dots_in[which], axis=0)
        return [
            jnp.sum(jnp.where(tile_lane[:1] == index, row, 0.0), axis=1, keepdims=True)
            for index in range(number)
        ]

    @pl.loop(0, size_x)
    def _(i):
        put_field(0, field0, i, sens[i] / diagonal(i))

    zero = jnp.zeros((8, 128), jnp.float32)
    sent = exchange(0, field0)

    def first(i, sums):
        image = apply(0, field0, i)
        image0[i] = image
        put_field(1, field1, i, image / diagonal(i))
        scaled = field0[i + 1]
        return (sums[0] + fold(sens[i] * scaled), sums[1] + fold(image * scaled))

    dots = lax.fori_loop(0, size_x, first, (zero, zero))
    send_dots(0, dots)
    sent = sent + exchange(1, field1)

    @pl.loop(0, size_x)
    def _(i):
        image = apply(1, field1, i)
        image1[i] = image
        put_field(2, field2, i, image / diagonal(i))

    sent = sent + exchange(2, field2)

    @pl.loop(0, size_x)
    def _(i):
        image2[i] = apply(2, field2, i)

    g0, k0 = take_dots(0, 2)
    s0 = g0 / k0

    def second(i, sums):
        w1, im0, im1 = field1[i + 1], image0[i], image1[i]
        z1 = field0[i + 1] - s0 * w1
        r1 = sens[i] - s0 * im0
        az1 = im0 - s0 * im1
        y1 = w1 - s0 * field2[i + 1]
        ay1 = im1 - s0 * image2[i]
        terms = (r1 * z1, z1 * az1, y1 * az1, az1 * w1, w1 * im0, y1 * ay1, y1 * im1, w1 * im1)
        return tuple(total + fold(term) for total, term in zip(sums, terms))

    dots = lax.fori_loop(0, size_x, second, (zero,) * 8)
    send_dots(1, dots)
    g1, c1, d1, d2, d3, e1, e2, e3 = take_dots(1, 8)
    b1 = g1 / g0
    s1 = g1 / (c1 - b1 * g1 / s0)
    d0 = -g1 / s0
    g2 = g1 - 2.0 * s1 * (c1 + b1 * d0) + s1 * s1 * (d1 + 2.0 * b1 * d2 + b1 * b1 * d3)
    g2 = jnp.maximum(g2, 0.0)
    c2 = c1 - 2.0 * s1 * (d1 + b1 * d2) + s1 * s1 * (e1 + 2.0 * b1 * e2 + b1 * b1 * e3)
    b2 = g2 / g1
    s2 = g2 / (c2 - b2 * g2 / s1)
    t1 = s0 + s1 * (1.0 + b1)
    weight0 = t1 + s2 * (1.0 + b2 * (1.0 + b1))
    weight1 = -(s1 * s0 + s2 * (t1 + b2 * s0))
    weight2 = s2 * s0 * s1

    @pl.loop(0, size_x)
    def _(i):
        filt[i] = weight0 * field0[i + 1] + weight1 * field1[i + 1] + weight2 * field2[i + 1]

    for copy, sends, _ in sent:
        pl.when(sends)(copy.wait_send)
    for which in range(2):
        whole = dots_in.at[which, pl.ds(0, count - 1)]
        pltpu.make_async_copy(whole, whole, dots_send.at[which]).wait()


def solution(mesh):
    n_x, n_y = mesh.shape["gx"], mesh.shape["gy"]

    def per_device(displacement, density, stiffness):
        size_x, size_y, size_z = density.shape
        block = (size_x, size_y, size_z)
        wide = pltpu.VMEM((size_x + 2, size_y, size_z), jnp.float32)
        same = pltpu.VMEM(block, jnp.float32)
        vmem = pl.BlockSpec(memory_space=pltpu.VMEM)
        return pl.pallas_call(
            functools.partial(kernel, n_x, n_y),
            out_shape=(jax.ShapeDtypeStruct(block, jnp.float32),) * 2,
            in_specs=[vmem, vmem, pl.BlockSpec(memory_space=pltpu.SMEM)],
            out_specs=(vmem, vmem),
            scratch_shapes=[
                pltpu.VMEM((4, 3, size_x + 1, size_y, size_z), jnp.float32),
                pltpu.VMEM((3, size_y, size_z), jnp.float32),
                pltpu.VMEM((3, size_x, size_z), jnp.float32),
                pltpu.VMEM((3, size_x, size_z), jnp.float32),
                pltpu.VMEM((8, size_z), jnp.float32),
                pltpu.VMEM((8, size_z), jnp.float32),
                wide, wide, wide, same, same, same,
                pltpu.VMEM((3, 2, size_x, size_z), jnp.float32),
                pltpu.VMEM((3, 2, size_x, size_z), jnp.float32),
                pltpu.VMEM((2, 1, 128), jnp.float32),
                pltpu.VMEM((2, n_x * n_y, 1, 128), jnp.float32),
                pltpu.SemaphoreType.DMA((3,)),
                pltpu.SemaphoreType.DMA((3,)),
                pltpu.SemaphoreType.DMA((3, 4)),
                pltpu.SemaphoreType.DMA((3, 4)),
                pltpu.SemaphoreType.DMA((2,)),
                pltpu.SemaphoreType.DMA((2,)),
            ],
            compiler_params=pltpu.CompilerParams(
                collective_id=0, has_side_effects=True, vmem_limit_bytes=48 * 1024 * 1024
            ),
        )(displacement, density, stiffness)

    return jax.shard_map(
        per_device,
        mesh=mesh,
        in_specs=(P(None, "gx", "gy", None), P("gx", "gy", None), P()),
        out_specs=(P("gx", "gy", None), P("gx", "gy", None)),
        check_vma=False,
    )
```

```python
import functools

import jax
import jax.numpy as jnp
from jax import lax
from jax.experimental import pallas as pl
from jax.experimental.pallas import tpu as pltpu
from jax.sharding import PartitionSpec as P

MESH = pl.DeviceIdType.MESH
penal = 3.0
e_min = 0.001
filter_weight = 2.0


def kernel(
    n_x, n_y,
    disp_in, dens_in, stiff_in,
    sens_out, filt_out,
    disp, dens, stiff, load_sems, sens, filt, store_sems,
    views, x_in, y_out, y_in, c_out, c_in,
    field0, field1, field2, image0, image1, image2, face_out, face_in, dots_out, dots_in,
    halo_send, halo_recv, face_send, face_recv, dots_send, dots_recv,
):
    size_x, size_y, size_z = dens.shape
    me_x, me_y = lax.axis_index("gx"), lax.axis_index("gy")
    me = me_x * n_y + me_y
    count = n_x * n_y
    has_xp, has_xn = me_x > 0, me_x < n_x - 1
    has_yp, has_yn = me_y > 0, me_y < n_y - 1

    def place(index):
        return {"gx": index // n_y, "gy": lax.rem(index, n_y)}

    loads = [
        pltpu.make_async_copy(disp_in, disp, load_sems.at[0]),
        pltpu.make_async_copy(stiff_in, stiff, load_sems.at[1]),
        pltpu.make_async_copy(dens_in, dens, load_sems.at[2]),
    ]
    for load in loads:
        load.start()
    barrier = pltpu.get_barrier_semaphore()

    @pl.loop(1, count)
    def _(offset):
        pl.semaphore_signal(
            barrier, inc=1, device_id=place(lax.rem(me + offset, count)), device_id_type=MESH
        )

    @pl.when(jnp.logical_not(has_xn))
    def _():
        x_in[...] = jnp.zeros_like(x_in)
        for field in (field0, field1, field2):
            field[size_x + 1] = jnp.zeros((size_y, size_z), jnp.float32)

    @pl.when(jnp.logical_not(has_xp))
    def _():
        for field in (field0, field1, field2):
            field[0] = jnp.zeros((size_y, size_z), jnp.float32)

    @pl.when(jnp.logical_not(has_yn))
    def _():
        y_in[...] = jnp.zeros_like(y_in)
        for step in range(3):
            face_in[step, 1] = jnp.zeros((size_x, size_z), jnp.float32)

    @pl.when(jnp.logical_not(has_yp))
    def _():
        for step in range(3):
            face_in[step, 0] = jnp.zeros((size_x, size_z), jnp.float32)

    @pl.when(jnp.logical_not(jnp.logical_and(has_xn, has_yn)))
    def _():
        c_in[...] = jnp.zeros_like(c_in)

    loads[0].wait()
    c_out[...] = jnp.zeros_like(c_out)
    for m in range(3):
        for i in range(size_x):
            y_out[m, i : i + 1, :] = disp[m, i, 0:1, :]
        c_out[m : m + 1, :] = disp[m, 0, 0:1, :]

    pl.semaphore_wait(barrier, count - 1)

    def remote(src, dst, send, recv, to_x, to_y):
        return pltpu.make_async_remote_copy(
            src_ref=src, dst_ref=dst, send_sem=send, recv_sem=recv,
            device_id={"gx": to_x, "gy": to_y}, device_id_type=MESH,
        )

    halo_x = remote(disp.at[:, 0], x_in, halo_send.at[0], halo_recv.at[0], me_x - 1, me_y)
    halo_y = remote(y_out, y_in, halo_send.at[1], halo_recv.at[1], me_x, me_y - 1)
    halo_c = remote(c_out, c_in, halo_send.at[2], halo_recv.at[2], me_x - 1, me_y - 1)
    halos = (
        (halo_x, has_xp, has_xn),
        (halo_y, has_yp, has_yn),
        (halo_c, jnp.logical_and(has_xp, has_yp), jnp.logical_and(has_xn, has_yn)),
    )
    for copy, sends, _ in halos:
        pl.when(sends)(copy.start)

    rows = lax.broadcasted_iota(jnp.int32, (size_y, size_z), 0)
    lanes = lax.broadcasted_iota(jnp.int32, (size_y, size_z), 1)

    def later_z(value):
        return jnp.where(lanes == size_z - 1, 0.0, pltpu.roll(value, size_z - 1, 1))

    def earlier_z(value):
        return jnp.where(lanes == 0, 0.0, pltpu.roll(value, 1, 1))

    def put_views(m, i, value, last_row):
        upper = pltpu.roll(value, size_y - 1, 0)
        if last_row is not None:
            upper = jnp.where(rows == size_y - 1, jnp.broadcast_to(last_row, value.shape), upper)
        views[0, m, i] = value
        views[1, m, i] = later_z(value)
        views[2, m, i] = upper
        views[3, m, i] = later_z(upper)

    @pl.loop(0, size_x)
    def _(i):
        for m in range(3):
            put_views(m, i, disp[m, i], None)

    def energy_block(i, start):
        def view(dof):
            a, b, c, m = dof // 12, dof // 6 % 2, dof // 3 % 2, dof % 3
            return views[2 * b + c, m, i + a, start : start + 8, :]

        energy = None
        for row in range(24):
            weighted = (0.5 * stiff[row, row]) * view(row)
            for col in range(row + 1, 24):
                weighted = weighted + stiff[row, col] * view(col)
            term = view(row) * weighted
            energy = term if energy is None else energy + term
        rho = dens[i, start : start + 8, :]
        sens[i, start : start + 8, :] = (-2.0 * penal * (1.0 - e_min)) * (rho * rho) * energy

    loads[1].wait()
    loads[2].wait()

    @pl.loop(0, size_x - 1)
    def _(i):
        energy_block(i, 0)

    for copy, sends, receives in halos:
        pl.when(receives)(copy.wait_recv)
    for m in range(3):
        put_views(m, size_x, x_in[m], c_in[m : m + 1, :])

    @pl.loop(0, size_x)
    def _(i):
        for m in range(3):
            last = y_in[m, pl.ds(i, 1), :]
            views[2, m, i, size_y - 1 : size_y, :] = last
            views[3, m, i, size_y - 1 : size_y, :] = jnp.where(
                lanes[:1] == size_z - 1, 0.0, pltpu.roll(last, size_z - 1, 1)
            )

    for start in range(8, size_y, 8):
        @pl.loop(0, size_x)
        def _(i):
            energy_block(i, start)

    energy_block(size_x - 1, 0)

    for copy, sends, _ in halos:
        pl.when(sends)(copy.wait_send)

    plane = 6.0 - (lanes == 0).astype(jnp.float32) - (lanes == size_z - 1).astype(jnp.float32)
    row_low = jnp.logical_and(rows == 0, jnp.logical_not(has_yp))
    row_high = jnp.logical_and(rows == size_y - 1, jnp.logical_not(has_yn))
    plane = plane - row_low.astype(jnp.float32) - row_high.astype(jnp.float32)

    def diagonal(i):
        at_low = jnp.logical_and(i == 0, jnp.logical_not(has_xp))
        at_high = jnp.logical_and(i == size_x - 1, jnp.logical_not(has_xn))
        missing = at_low.astype(jnp.float32) + at_high.astype(jnp.float32)
        return 1.0 + filter_weight * (plane - missing)

    def put_field(step, field, i, value):
        field[i + 1] = value
        face_out[step, 0, pl.ds(i, 1), :] = value[0:1]
        face_out[step, 1, pl.ds(i, 1), :] = value[size_y - 1 : size_y]

    def faces(step, field):
        return (
            (remote(field.at[1], field.at[size_x + 1], face_send.at[step, 0],
                    face_recv.at[step, 0], me_x - 1, me_y), has_xp, has_xn),
            (remote(field.at[size_x], field.at[0], face_send.at[step, 1],
                    face_recv.at[step, 1], me_x + 1, me_y), has_xn, has_xp),
            (remote(face_out.at[step, 0], face_in.at[step, 1], face_send.at[step, 2],
                    face_recv.at[step, 2], me_x, me_y - 1), has_yp, has_yn),
            (remote(face_out.at[step, 1], face_in.at[step, 0], face_send.at[step, 3],
                    face_recv.at[step, 3], me_x, me_y + 1), has_yn, has_yp),
        )

    def start_exchange(step, field):
        copies = faces(step, field)
        for copy, sends, _ in copies:
            pl.when(sends)(copy.start)
        return copies

    def finish_exchange(copies):
        for copy, _, receives in copies:
            pl.when(receives)(copy.wait_recv)

    def apply(step, field, i):
        value = field[i + 1]
        below = jnp.where(rows == 0, jnp.broadcast_to(face_in[step, 0, pl.ds(i, 1), :], value.shape),
                          pltpu.roll(value, 1, 0))
        above = jnp.where(rows == size_y - 1,
                          jnp.broadcast_to(face_in[step, 1, pl.ds(i, 1), :], value.shape),
                          pltpu.roll(value, size_y - 1, 0))
        beside = field[i] + field[i + 2] + below + above + later_z(value) + earlier_z(value)
        return diagonal(i) * value - filter_weight * beside

    def fold(value):
        part = value[0:8]
        for start in range(8, size_y, 8):
            part = part + value[start : start + 8]
        total = part[:, 0:128]
        for start in range(128, size_z, 128):
            total = total + part[:, start : start + 128]
        return total

    tile_row = lax.broadcasted_iota(jnp.int32, (8, 128), 0)
    tile_lane = lax.broadcasted_iota(jnp.int32, (8, 128), 1)

    def send_dots(which, parts):
        packed = jnp.zeros((8, 128), jnp.float32)
        for index, part in enumerate(parts):
            packed = packed + jnp.where(
                tile_row == index, jnp.broadcast_to(jnp.sum(part, axis=0, keepdims=True), (8, 128)), 0.0
            )
        totals = jnp.broadcast_to(jnp.sum(packed, axis=1, keepdims=True), (8, 128))
        row = jnp.sum(jnp.where(tile_row == tile_lane, totals, 0.0), axis=0, keepdims=True)
        dots_out[which] = row
        dots_in[which, count - 1] = row

        @pl.loop(1, count)
        def _(offset):
            to = place(lax.rem(me + offset, count))
            remote(dots_out.at[which], dots_in.at[which, offset - 1], dots_send.at[which],
                   dots_recv.at[which], to["gx"], to["gy"]).start()

    def take_dots(which, number):
        whole = dots_in.at[which, pl.ds(0, count - 1)]
        pltpu.make_async_copy(whole, whole, dots_recv.at[which]).wait()
        row = jnp.sum(dots_in[which], axis=0)
        return [
            jnp.sum(jnp.where(tile_lane[:1] == index, row, 0.0), axis=1, keepdims=True)
            for index in range(number)
        ]

    @pl.loop(0, size_x)
    def _(i):
        put_field(0, field0, i, sens[i] / diagonal(i))

    zero = jnp.zeros((8, 128), jnp.float32)
    sent0 = start_exchange(0, field0)
    store_sens = pltpu.make_async_copy(sens, sens_out, store_sems.at[0])
    store_sens.start()
    finish_exchange(sent0)

    def first(i, sums):
        image = apply(0, field0, i)
        image0[i] = image
        put_field(1, field1, i, image / diagonal(i))
        scaled = field0[i + 1]
        return (sums[0] + fold(sens[i] * scaled), sums[1] + fold(image * scaled))

    dots = lax.fori_loop(0, size_x, first, (zero, zero))
    sent1 = start_exchange(1, field1)
    send_dots(0, dots)
    finish_exchange(sent1)

    @pl.loop(0, size_x)
    def _(i):
        image = apply(1, field1, i)
        image1[i] = image
        put_field(2, field2, i, image / diagonal(i))

    sent2 = start_exchange(2, field2)
    finish_exchange(sent2)

    @pl.loop(0, size_x)
    def _(i):
        image2[i] = apply(2, field2, i)

    g0, k0 = take_dots(0, 2)
    s0 = g0 / k0

    def second(i, sums):
        w1, im0, im1 = field1[i + 1], image0[i], image1[i]
        z1 = field0[i + 1] - s0 * w1
        r1 = sens[i] - s0 * im0
        az1 = im0 - s0 * im1
        y1 = w1 - s0 * field2[i + 1]
        ay1 = im1 - s0 * image2[i]
        terms = (r1 * z1, z1 * az1, y1 * az1, az1 * w1, w1 * im0, y1 * ay1, y1 * im1, w1 * im1)
        return tuple(total + fold(term) for total, term in zip(sums, terms))

    dots = lax.fori_loop(0, size_x, second, (zero,) * 8)
    send_dots(1, dots)
    g1, c1, d1, d2, d3, e1, e2, e3 = take_dots(1, 8)
    b1 = g1 / g0
    s1 = g1 / (c1 - b1 * g1 / s0)
    d0 = -g1 / s0
    g2 = g1 - 2.0 * s1 * (c1 + b1 * d0) + s1 * s1 * (d1 + 2.0 * b1 * d2 + b1 * b1 * d3)
    g2 = jnp.maximum(g2, 0.0)
    c2 = c1 - 2.0 * s1 * (d1 + b1 * d2) + s1 * s1 * (e1 + 2.0 * b1 * e2 + b1 * b1 * e3)
    b2 = g2 / g1
    s2 = g2 / (c2 - b2 * g2 / s1)
    t1 = s0 + s1 * (1.0 + b1)
    weight0 = t1 + s2 * (1.0 + b2 * (1.0 + b1))
    weight1 = -(s1 * s0 + s2 * (t1 + b2 * s0))
    weight2 = s2 * s0 * s1

    @pl.loop(0, size_x)
    def _(i):
        filt[i] = weight0 * field0[i + 1] + weight1 * field1[i + 1] + weight2 * field2[i + 1]

    store_filt = pltpu.make_async_copy(filt, filt_out, store_sems.at[1])
    store_filt.start()
    for copy, sends, _ in sent0 + sent1 + sent2:
        pl.when(sends)(copy.wait_send)
    for which in range(2):
        whole = dots_in.at[which, pl.ds(0, count - 1)]
        pltpu.make_async_copy(whole, whole, dots_send.at[which]).wait()
    store_sens.wait()
    store_filt.wait()


def solution(mesh):
    n_x, n_y = mesh.shape["gx"], mesh.shape["gy"]

    def per_device(displacement, density, stiffness):
        size_x, size_y, size_z = density.shape
        block = (size_x, size_y, size_z)
        wide = pltpu.VMEM((size_x + 2, size_y, size_z), jnp.float32)
        same = pltpu.VMEM(block, jnp.float32)
        return pl.pallas_call(
            functools.partial(kernel, n_x, n_y),
            out_shape=(jax.ShapeDtypeStruct(block, jnp.float32),) * 2,
            in_specs=[pl.BlockSpec(memory_space=pltpu.HBM)] * 3,
            out_specs=(pl.BlockSpec(memory_space=pltpu.HBM),) * 2,
            scratch_shapes=[
                pltpu.VMEM(displacement.shape, jnp.float32),
                same,
                pltpu.SMEM(stiffness.shape, jnp.float32),
                pltpu.SemaphoreType.DMA((3,)),
                same,
                same,
                pltpu.SemaphoreType.DMA((2,)),
                pltpu.VMEM((4, 3, size_x + 1, size_y, size_z), jnp.float32),
                pltpu.VMEM((3, size_y, size_z), jnp.float32),
                pltpu.VMEM((3, size_x, size_z), jnp.float32),
                pltpu.VMEM((3, size_x, size_z), jnp.float32),
                pltpu.VMEM((8, size_z), jnp.float32),
                pltpu.VMEM((8, size_z), jnp.float32),
                wide, wide, wide, same, same, same,
                pltpu.VMEM((3, 2, size_x, size_z), jnp.float32),
                pltpu.VMEM((3, 2, size_x, size_z), jnp.float32),
                pltpu.VMEM((2, 1, 128), jnp.float32),
                pltpu.VMEM((2, n_x * n_y, 1, 128), jnp.float32),
                pltpu.SemaphoreType.DMA((3,)),
                pltpu.SemaphoreType.DMA((3,)),
                pltpu.SemaphoreType.DMA((3, 4)),
                pltpu.SemaphoreType.DMA((3, 4)),
                pltpu.SemaphoreType.DMA((2,)),
                pltpu.SemaphoreType.DMA((2,)),
            ],
            compiler_params=pltpu.CompilerParams(
                collective_id=0, has_side_effects=True, vmem_limit_bytes=62 * 1024 * 1024
            ),
        )(displacement, density, stiffness)

    return jax.shard_map(
        per_device,
        mesh=mesh,
        in_specs=(P(None, "gx", "gy", None), P("gx", "gy", None), P()),
        out_specs=(P("gx", "gy", None), P("gx", "gy", None)),
        check_vma=False,
    )
```

```python
import functools

import jax
import jax.numpy as jnp
from jax import lax
from jax.experimental import pallas as pl
from jax.experimental.pallas import tpu as pltpu
from jax.sharding import PartitionSpec as P

MESH = pl.DeviceIdType.MESH
penal = 3.0
e_min = 0.001
filter_weight = 2.0


def kernel(
    n_x, n_y,
    disp_in, dens_in, stiff_in,
    sens_out, filt_out,
    disp, dens, stiff, load_sems, sens, filt, store_sems,
    views, x_in, y_out, y_in, c_out, c_in,
    field0, field1, field2, image0, image1, image2, face_out, face_in, dots_out, dots_in,
    halo_send, halo_recv, face_send, face_recv, dots_send, dots_recv,
):
    size_x, size_y, size_z = dens.shape
    me_x, me_y = lax.axis_index("gx"), lax.axis_index("gy")
    me = me_x * n_y + me_y
    count = n_x * n_y
    has_xp, has_xn = me_x > 0, me_x < n_x - 1
    has_yp, has_yn = me_y > 0, me_y < n_y - 1

    def place(index):
        return {"gx": index // n_y, "gy": lax.rem(index, n_y)}

    loads = [
        pltpu.make_async_copy(disp_in, disp, load_sems.at[0]),
        pltpu.make_async_copy(stiff_in, stiff, load_sems.at[1]),
        pltpu.make_async_copy(dens_in, dens, load_sems.at[2]),
    ]
    for load in loads:
        load.start()
    barrier = pltpu.get_barrier_semaphore()

    @pl.loop(1, count)
    def _(offset):
        pl.semaphore_signal(
            barrier, inc=1, device_id=place(lax.rem(me + offset, count)), device_id_type=MESH
        )

    @pl.when(jnp.logical_not(has_xn))
    def _():
        x_in[...] = jnp.zeros_like(x_in)
        for field in (field0, field1, field2):
            field[size_x + 1] = jnp.zeros((size_y, size_z), jnp.float32)

    @pl.when(jnp.logical_not(has_xp))
    def _():
        for field in (field0, field1, field2):
            field[0] = jnp.zeros((size_y, size_z), jnp.float32)

    @pl.when(jnp.logical_not(has_yn))
    def _():
        y_in[...] = jnp.zeros_like(y_in)
        for step in range(3):
            face_in[step, 1] = jnp.zeros((size_x, size_z), jnp.float32)

    @pl.when(jnp.logical_not(has_yp))
    def _():
        for step in range(3):
            face_in[step, 0] = jnp.zeros((size_x, size_z), jnp.float32)

    @pl.when(jnp.logical_not(jnp.logical_and(has_xn, has_yn)))
    def _():
        c_in[...] = jnp.zeros_like(c_in)

    loads[0].wait()
    c_out[...] = jnp.zeros_like(c_out)
    for m in range(3):
        for i in range(size_x):
            y_out[m, i : i + 1, :] = disp[m, i, 0:1, :]
        c_out[m : m + 1, :] = disp[m, 0, 0:1, :]

    pl.semaphore_wait(barrier, count - 1)

    def remote(src, dst, send, recv, to_x, to_y):
        return pltpu.make_async_remote_copy(
            src_ref=src, dst_ref=dst, send_sem=send, recv_sem=recv,
            device_id={"gx": to_x, "gy": to_y}, device_id_type=MESH,
        )

    halo_x = remote(disp.at[:, 0], x_in, halo_send.at[0], halo_recv.at[0], me_x - 1, me_y)
    halo_y = remote(y_out, y_in, halo_send.at[1], halo_recv.at[1], me_x, me_y - 1)
    halo_c = remote(c_out, c_in, halo_send.at[2], halo_recv.at[2], me_x - 1, me_y - 1)
    halos = (
        (halo_x, has_xp, has_xn),
        (halo_y, has_yp, has_yn),
        (halo_c, jnp.logical_and(has_xp, has_yp), jnp.logical_and(has_xn, has_yn)),
    )
    for copy, sends, _ in halos:
        pl.when(sends)(copy.start)

    rows = lax.broadcasted_iota(jnp.int32, (size_y, size_z), 0)
    lanes = lax.broadcasted_iota(jnp.int32, (size_y, size_z), 1)

    def later_z(value):
        return jnp.where(lanes == size_z - 1, 0.0, pltpu.roll(value, size_z - 1, 1))

    def earlier_z(value):
        return jnp.where(lanes == 0, 0.0, pltpu.roll(value, 1, 1))

    def put_views(m, i, value, last_row):
        upper = pltpu.roll(value, size_y - 1, 0)
        if last_row is not None:
            upper = jnp.where(rows == size_y - 1, jnp.broadcast_to(last_row, value.shape), upper)
        views[0, m, i] = value
        views[1, m, i] = later_z(value)
        views[2, m, i] = upper
        views[3, m, i] = later_z(upper)

    @pl.loop(0, size_x, unroll=True)
    def _(i):
        for m in range(3):
            put_views(m, i, disp[m, i], None)

    def energy_block(i, start):
        def view(dof):
            a, b, c, m = dof // 12, dof // 6 % 2, dof // 3 % 2, dof % 3
            return views[2 * b + c, m, i + a, start : start + 8, :]

        energy = None
        for row in range(24):
            weighted = (0.5 * stiff[row, row]) * view(row)
            for col in range(row + 1, 24):
                weighted = weighted + stiff[row, col] * view(col)
            term = view(row) * weighted
            energy = term if energy is None else energy + term
        rho = dens[i, start : start + 8, :]
        sens[i, start : start + 8, :] = (-2.0 * penal * (1.0 - e_min)) * (rho * rho) * energy

    loads[1].wait()
    loads[2].wait()

    @pl.loop(0, size_x - 1)
    def _(i):
        energy_block(i, 0)

    for copy, sends, receives in halos:
        pl.when(receives)(copy.wait_recv)
    for m in range(3):
        put_views(m, size_x, x_in[m], c_in[m : m + 1, :])

    @pl.loop(0, size_x, unroll=True)
    def _(i):
        for m in range(3):
            last = y_in[m, pl.ds(i, 1), :]
            views[2, m, i, size_y - 1 : size_y, :] = last
            views[3, m, i, size_y - 1 : size_y, :] = jnp.where(
                lanes[:1] == size_z - 1, 0.0, pltpu.roll(last, size_z - 1, 1)
            )

    for start in range(8, size_y, 8):
        @pl.loop(0, size_x)
        def _(i):
            energy_block(i, start)

    energy_block(size_x - 1, 0)

    for copy, sends, _ in halos:
        pl.when(sends)(copy.wait_send)

    plane = 6.0 - (lanes == 0).astype(jnp.float32) - (lanes == size_z - 1).astype(jnp.float32)
    row_low = jnp.logical_and(rows == 0, jnp.logical_not(has_yp))
    row_high = jnp.logical_and(rows == size_y - 1, jnp.logical_not(has_yn))
    plane = plane - row_low.astype(jnp.float32) - row_high.astype(jnp.float32)

    def diagonal(i):
        at_low = jnp.logical_and(i == 0, jnp.logical_not(has_xp))
        at_high = jnp.logical_and(i == size_x - 1, jnp.logical_not(has_xn))
        missing = at_low.astype(jnp.float32) + at_high.astype(jnp.float32)
        return 1.0 + filter_weight * (plane - missing)

    def put_field(step, field, i, value):
        field[i + 1] = value
        face_out[step, 0, pl.ds(i, 1), :] = value[0:1]
        face_out[step, 1, pl.ds(i, 1), :] = value[size_y - 1 : size_y]

    def faces(step, field):
        return (
            (remote(field.at[1], field.at[size_x + 1], face_send.at[step, 0],
                    face_recv.at[step, 0], me_x - 1, me_y), has_xp, has_xn),
            (remote(field.at[size_x], field.at[0], face_send.at[step, 1],
                    face_recv.at[step, 1], me_x + 1, me_y), has_xn, has_xp),
            (remote(face_out.at[step, 0], face_in.at[step, 1], face_send.at[step, 2],
                    face_recv.at[step, 2], me_x, me_y - 1), has_yp, has_yn),
            (remote(face_out.at[step, 1], face_in.at[step, 0], face_send.at[step, 3],
                    face_recv.at[step, 3], me_x, me_y + 1), has_yn, has_yp),
        )

    def start_exchange(step, field):
        copies = faces(step, field)
        for copy, sends, _ in copies:
            pl.when(sends)(copy.start)
        return copies

    def finish_exchange(copies):
        for copy, _, receives in copies:
            pl.when(receives)(copy.wait_recv)

    def apply(step, field, i):
        value = field[i + 1]
        below = jnp.where(rows == 0, jnp.broadcast_to(face_in[step, 0, pl.ds(i, 1), :], value.shape),
                          pltpu.roll(value, 1, 0))
        above = jnp.where(rows == size_y - 1,
                          jnp.broadcast_to(face_in[step, 1, pl.ds(i, 1), :], value.shape),
                          pltpu.roll(value, size_y - 1, 0))
        beside = field[i] + field[i + 2] + below + above + later_z(value) + earlier_z(value)
        return diagonal(i) * value - filter_weight * beside

    def fold(value):
        part = value[0:8]
        for start in range(8, size_y, 8):
            part = part + value[start : start + 8]
        total = part[:, 0:128]
        for start in range(128, size_z, 128):
            total = total + part[:, start : start + 128]
        return total

    tile_row = lax.broadcasted_iota(jnp.int32, (8, 128), 0)
    tile_lane = lax.broadcasted_iota(jnp.int32, (8, 128), 1)

    def send_dots(which, parts):
        packed = jnp.zeros((8, 128), jnp.float32)
        for index, part in enumerate(parts):
            packed = packed + jnp.where(
                tile_row == index, jnp.broadcast_to(jnp.sum(part, axis=0, keepdims=True), (8, 128)), 0.0
            )
        totals = jnp.broadcast_to(jnp.sum(packed, axis=1, keepdims=True), (8, 128))
        row = jnp.sum(jnp.where(tile_row == tile_lane, totals, 0.0), axis=0, keepdims=True)
        dots_out[which] = row
        dots_in[which, count - 1] = row

        @pl.loop(1, count)
        def _(offset):
            to = place(lax.rem(me + offset, count))
            remote(dots_out.at[which], dots_in.at[which, offset - 1], dots_send.at[which],
                   dots_recv.at[which], to["gx"], to["gy"]).start()

    def take_dots(which, number):
        whole = dots_in.at[which, pl.ds(0, count - 1)]
        pltpu.make_async_copy(whole, whole, dots_recv.at[which]).wait()
        row = jnp.sum(dots_in[which], axis=0)
        return [
            jnp.sum(jnp.where(tile_lane[:1] == index, row, 0.0), axis=1, keepdims=True)
            for index in range(number)
        ]

    @pl.loop(0, size_x, unroll=True)
    def _(i):
        put_field(0, field0, i, sens[i] / diagonal(i))

    zero = jnp.zeros((8, 128), jnp.float32)
    sent0 = start_exchange(0, field0)
    store_sens = pltpu.make_async_copy(sens, sens_out, store_sems.at[0])
    store_sens.start()
    finish_exchange(sent0)

    def first(i, sums):
        image = apply(0, field0, i)
        image0[i] = image
        put_field(1, field1, i, image / diagonal(i))
        scaled = field0[i + 1]
        return (sums[0] + fold(sens[i] * scaled), sums[1] + fold(image * scaled))

    dots = lax.fori_loop(0, size_x, first, (zero, zero), unroll=True)
    sent1 = start_exchange(1, field1)
    send_dots(0, dots)
    finish_exchange(sent1)

    @pl.loop(0, size_x, unroll=True)
    def _(i):
        image = apply(1, field1, i)
        image1[i] = image
        put_field(2, field2, i, image / diagonal(i))

    sent2 = start_exchange(2, field2)
    finish_exchange(sent2)

    @pl.loop(0, size_x, unroll=True)
    def _(i):
        image2[i] = apply(2, field2, i)

    g0, k0 = take_dots(0, 2)
    s0 = g0 / k0

    def second(i, sums):
        w1, im0, im1 = field1[i + 1], image0[i], image1[i]
        z1 = field0[i + 1] - s0 * w1
        r1 = sens[i] - s0 * im0
        az1 = im0 - s0 * im1
        y1 = w1 - s0 * field2[i + 1]
        ay1 = im1 - s0 * image2[i]
        terms = (r1 * z1, z1 * az1, y1 * az1, az1 * w1, w1 * im0, y1 * ay1, y1 * im1, w1 * im1)
        return tuple(total + fold(term) for total, term in zip(sums, terms))

    dots = lax.fori_loop(0, size_x, second, (zero,) * 8, unroll=True)
    send_dots(1, dots)
    g1, c1, d1, d2, d3, e1, e2, e3 = take_dots(1, 8)
    b1 = g1 / g0
    s1 = g1 / (c1 - b1 * g1 / s0)
    d0 = -g1 / s0
    g2 = g1 - 2.0 * s1 * (c1 + b1 * d0) + s1 * s1 * (d1 + 2.0 * b1 * d2 + b1 * b1 * d3)
    g2 = jnp.maximum(g2, 0.0)
    c2 = c1 - 2.0 * s1 * (d1 + b1 * d2) + s1 * s1 * (e1 + 2.0 * b1 * e2 + b1 * b1 * e3)
    b2 = g2 / g1
    s2 = g2 / (c2 - b2 * g2 / s1)
    t1 = s0 + s1 * (1.0 + b1)
    weight0 = t1 + s2 * (1.0 + b2 * (1.0 + b1))
    weight1 = -(s1 * s0 + s2 * (t1 + b2 * s0))
    weight2 = s2 * s0 * s1

    @pl.loop(0, size_x, unroll=True)
    def _(i):
        filt[i] = weight0 * field0[i + 1] + weight1 * field1[i + 1] + weight2 * field2[i + 1]

    store_filt = pltpu.make_async_copy(filt, filt_out, store_sems.at[1])
    store_filt.start()
    for copy, sends, _ in sent0 + sent1 + sent2:
        pl.when(sends)(copy.wait_send)
    for which in range(2):
        whole = dots_in.at[which, pl.ds(0, count - 1)]
        pltpu.make_async_copy(whole, whole, dots_send.at[which]).wait()
    store_sens.wait()
    store_filt.wait()


def solution(mesh):
    n_x, n_y = mesh.shape["gx"], mesh.shape["gy"]

    def per_device(displacement, density, stiffness):
        size_x, size_y, size_z = density.shape
        block = (size_x, size_y, size_z)
        wide = pltpu.VMEM((size_x + 2, size_y, size_z), jnp.float32)
        same = pltpu.VMEM(block, jnp.float32)
        return pl.pallas_call(
            functools.partial(kernel, n_x, n_y),
            out_shape=(jax.ShapeDtypeStruct(block, jnp.float32),) * 2,
            in_specs=[pl.BlockSpec(memory_space=pltpu.HBM)] * 3,
            out_specs=(pl.BlockSpec(memory_space=pltpu.HBM),) * 2,
            scratch_shapes=[
                pltpu.VMEM(displacement.shape, jnp.float32),
                same,
                pltpu.SMEM(stiffness.shape, jnp.float32),
                pltpu.SemaphoreType.DMA((3,)),
                same,
                same,
                pltpu.SemaphoreType.DMA((2,)),
                pltpu.VMEM((4, 3, size_x + 1, size_y, size_z), jnp.float32),
                pltpu.VMEM((3, size_y, size_z), jnp.float32),
                pltpu.VMEM((3, size_x, size_z), jnp.float32),
                pltpu.VMEM((3, size_x, size_z), jnp.float32),
                pltpu.VMEM((8, size_z), jnp.float32),
                pltpu.VMEM((8, size_z), jnp.float32),
                wide, wide, wide, same, same, same,
                pltpu.VMEM((3, 2, size_x, size_z), jnp.float32),
                pltpu.VMEM((3, 2, size_x, size_z), jnp.float32),
                pltpu.VMEM((2, 1, 128), jnp.float32),
                pltpu.VMEM((2, n_x * n_y, 1, 128), jnp.float32),
                pltpu.SemaphoreType.DMA((3,)),
                pltpu.SemaphoreType.DMA((3,)),
                pltpu.SemaphoreType.DMA((3, 4)),
                pltpu.SemaphoreType.DMA((3, 4)),
                pltpu.SemaphoreType.DMA((2,)),
                pltpu.SemaphoreType.DMA((2,)),
            ],
            compiler_params=pltpu.CompilerParams(
                collective_id=0, has_side_effects=True, vmem_limit_bytes=62 * 1024 * 1024
            ),
        )(displacement, density, stiffness)

    return jax.shard_map(
        per_device,
        mesh=mesh,
        in_specs=(P(None, "gx", "gy", None), P("gx", "gy", None), P()),
        out_specs=(P("gx", "gy", None), P("gx", "gy", None)),
        check_vma=False,
    )
```

```python
import functools

import jax
import jax.numpy as jnp
from jax import lax
from jax.experimental import pallas as pl
from jax.experimental.pallas import tpu as pltpu
from jax.sharding import PartitionSpec as P

MESH = pl.DeviceIdType.MESH
penal = 3.0
e_min = 0.001
filter_weight = 2.0


def kernel(
    n_x, n_y,
    disp_in, dens_in, stiff_in,
    sens_out, filt_out,
    disp, dens, stiff, load_sems, sens, filt, store_sems,
    views, x_in, y_out, y_in, c_out, c_in,
    field0, field1, field2, image0, image1, image2, face_out, face_in, dots_out, dots_in,
    halo_send, halo_recv, face_send, face_recv, dots_send, dots_recv,
):
    size_x, size_y, size_z = dens.shape
    me_x, me_y = lax.axis_index("gx"), lax.axis_index("gy")
    me = me_x * n_y + me_y
    count = n_x * n_y
    has_xp, has_xn = me_x > 0, me_x < n_x - 1
    has_yp, has_yn = me_y > 0, me_y < n_y - 1

    def place(index):
        return {"gx": index // n_y, "gy": lax.rem(index, n_y)}

    loads = [
        pltpu.make_async_copy(disp_in, disp, load_sems.at[0]),
        pltpu.make_async_copy(stiff_in, stiff, load_sems.at[1]),
        pltpu.make_async_copy(dens_in, dens, load_sems.at[2]),
    ]
    for load in loads:
        load.start()
    barrier = pltpu.get_barrier_semaphore()

    @pl.loop(1, count, unroll=4)
    def _(offset):
        pl.semaphore_signal(
            barrier, inc=1, device_id=place(lax.rem(me + offset, count)), device_id_type=MESH
        )

    @pl.when(jnp.logical_not(has_xn))
    def _():
        x_in[...] = jnp.zeros_like(x_in)
        for field in (field0, field1, field2):
            field[size_x + 1] = jnp.zeros((size_y, size_z), jnp.float32)

    @pl.when(jnp.logical_not(has_xp))
    def _():
        for field in (field0, field1, field2):
            field[0] = jnp.zeros((size_y, size_z), jnp.float32)

    @pl.when(jnp.logical_not(has_yn))
    def _():
        y_in[...] = jnp.zeros_like(y_in)
        for step in range(3):
            face_in[step, 1] = jnp.zeros((size_x, size_z), jnp.float32)

    @pl.when(jnp.logical_not(has_yp))
    def _():
        for step in range(3):
            face_in[step, 0] = jnp.zeros((size_x, size_z), jnp.float32)

    @pl.when(jnp.logical_not(jnp.logical_and(has_xn, has_yn)))
    def _():
        c_in[...] = jnp.zeros_like(c_in)

    loads[0].wait()
    pl.semaphore_wait(barrier, count - 1)

    def remote(src, dst, send, recv, to_x, to_y):
        return pltpu.make_async_remote_copy(
            src_ref=src, dst_ref=dst, send_sem=send, recv_sem=recv,
            device_id={"gx": to_x, "gy": to_y}, device_id_type=MESH,
        )

    halo_x = remote(disp.at[:, 0], x_in, halo_send.at[0], halo_recv.at[0], me_x - 1, me_y)
    halo_y = remote(y_out, y_in, halo_send.at[1], halo_recv.at[1], me_x, me_y - 1)
    halo_c = remote(c_out, c_in, halo_send.at[2], halo_recv.at[2], me_x - 1, me_y - 1)
    halos = (
        (halo_x, has_xp, has_xn),
        (halo_y, has_yp, has_yn),
        (halo_c, jnp.logical_and(has_xp, has_yp), jnp.logical_and(has_xn, has_yn)),
    )
    pl.when(has_xp)(halo_x.start)
    c_out[...] = jnp.zeros_like(c_out)
    for m in range(3):
        for i in range(size_x):
            y_out[m, i : i + 1, :] = disp[m, i, 0:1, :]
        c_out[m : m + 1, :] = disp[m, 0, 0:1, :]

    for copy, sends, _ in halos[1:]:
        pl.when(sends)(copy.start)

    rows = lax.broadcasted_iota(jnp.int32, (size_y, size_z), 0)
    lanes = lax.broadcasted_iota(jnp.int32, (size_y, size_z), 1)

    def later_z(value):
        return jnp.where(lanes == size_z - 1, 0.0, pltpu.roll(value, size_z - 1, 1))

    def earlier_z(value):
        return jnp.where(lanes == 0, 0.0, pltpu.roll(value, 1, 1))

    def put_views(m, i, value, last_row):
        upper = pltpu.roll(value, size_y - 1, 0)
        if last_row is not None:
            upper = jnp.where(rows == size_y - 1, jnp.broadcast_to(last_row, value.shape), upper)
        views[0, m, i] = value
        views[1, m, i] = later_z(value)
        views[2, m, i] = upper
        views[3, m, i] = later_z(upper)

    @pl.loop(0, size_x, unroll=True)
    def _(i):
        for m in range(3):
            put_views(m, i, disp[m, i], None)

    def energy_block(i, start):
        def view(dof):
            a, b, c, m = dof // 12, dof // 6 % 2, dof // 3 % 2, dof % 3
            return views[2 * b + c, m, i + a, start : start + 8, :]

        energy = None
        for row in range(24):
            weighted = (0.5 * stiff[row, row]) * view(row)
            for col in range(row + 1, 24):
                weighted = weighted + stiff[row, col] * view(col)
            term = view(row) * weighted
            energy = term if energy is None else energy + term
        rho = dens[i, start : start + 8, :]
        sens[i, start : start + 8, :] = (-2.0 * penal * (1.0 - e_min)) * (rho * rho) * energy

    loads[1].wait()
    loads[2].wait()

    @pl.loop(0, size_x - 1)
    def _(i):
        energy_block(i, 0)

    for copy, sends, receives in halos:
        pl.when(receives)(copy.wait_recv)
    for m in range(3):
        put_views(m, size_x, x_in[m], c_in[m : m + 1, :])

    @pl.loop(0, size_x, unroll=True)
    def _(i):
        for m in range(3):
            last = y_in[m, pl.ds(i, 1), :]
            views[2, m, i, size_y - 1 : size_y, :] = last
            views[3, m, i, size_y - 1 : size_y, :] = jnp.where(
                lanes[:1] == size_z - 1, 0.0, pltpu.roll(last, size_z - 1, 1)
            )

    for start in range(8, size_y, 8):
        @pl.loop(0, size_x)
        def _(i):
            energy_block(i, start)

    energy_block(size_x - 1, 0)

    for copy, sends, _ in halos:
        pl.when(sends)(copy.wait_send)

    plane = 6.0 - (lanes == 0).astype(jnp.float32) - (lanes == size_z - 1).astype(jnp.float32)
    row_low = jnp.logical_and(rows == 0, jnp.logical_not(has_yp))
    row_high = jnp.logical_and(rows == size_y - 1, jnp.logical_not(has_yn))
    plane = plane - row_low.astype(jnp.float32) - row_high.astype(jnp.float32)

    def diagonal(i):
        at_low = jnp.logical_and(i == 0, jnp.logical_not(has_xp))
        at_high = jnp.logical_and(i == size_x - 1, jnp.logical_not(has_xn))
        missing = at_low.astype(jnp.float32) + at_high.astype(jnp.float32)
        return 1.0 + filter_weight * (plane - missing)

    def put_field(step, field, i, value):
        field[i + 1] = value
        face_out[step, 0, pl.ds(i, 1), :] = value[0:1]
        face_out[step, 1, pl.ds(i, 1), :] = value[size_y - 1 : size_y]

    def faces(step, field):
        return (
            (remote(field.at[1], field.at[size_x + 1], face_send.at[step, 0],
                    face_recv.at[step, 0], me_x - 1, me_y), has_xp, has_xn),
            (remote(field.at[size_x], field.at[0], face_send.at[step, 1],
                    face_recv.at[step, 1], me_x + 1, me_y), has_xn, has_xp),
            (remote(face_out.at[step, 0], face_in.at[step, 1], face_send.at[step, 2],
                    face_recv.at[step, 2], me_x, me_y - 1), has_yp, has_yn),
            (remote(face_out.at[step, 1], face_in.at[step, 0], face_send.at[step, 3],
                    face_recv.at[step, 3], me_x, me_y + 1), has_yn, has_yp),
        )

    def start_exchange(step, field):
        copies = faces(step, field)
        for copy, sends, _ in copies:
            pl.when(sends)(copy.start)
        return copies

    def finish_exchange(copies):
        for copy, _, receives in copies:
            pl.when(receives)(copy.wait_recv)

    def apply(step, field, i):
        value = field[i + 1]
        below = jnp.where(rows == 0, jnp.broadcast_to(face_in[step, 0, pl.ds(i, 1), :], value.shape),
                          pltpu.roll(value, 1, 0))
        above = jnp.where(rows == size_y - 1,
                          jnp.broadcast_to(face_in[step, 1, pl.ds(i, 1), :], value.shape),
                          pltpu.roll(value, size_y - 1, 0))
        beside = field[i] + field[i + 2] + below + above + later_z(value) + earlier_z(value)
        return diagonal(i) * value - filter_weight * beside

    def fold(value):
        part = value[0:8]
        for start in range(8, size_y, 8):
            part = part + value[start : start + 8]
        total = part[:, 0:128]
        for start in range(128, size_z, 128):
            total = total + part[:, start : start + 128]
        return total

    tile_row = lax.broadcasted_iota(jnp.int32, (8, 128), 0)
    tile_lane = lax.broadcasted_iota(jnp.int32, (8, 128), 1)

    def send_dots(which, parts):
        packed = jnp.zeros((8, 128), jnp.float32)
        for index, part in enumerate(parts):
            packed = packed + jnp.where(
                tile_row == index, jnp.broadcast_to(jnp.sum(part, axis=0, keepdims=True), (8, 128)), 0.0
            )
        totals = jnp.broadcast_to(jnp.sum(packed, axis=1, keepdims=True), (8, 128))
        row = jnp.sum(jnp.where(tile_row == tile_lane, totals, 0.0), axis=0, keepdims=True)
        dots_out[which] = row
        dots_in[which, count - 1] = row

        @pl.loop(1, count, unroll=4)
        def _(offset):
            to = place(lax.rem(me + offset, count))
            remote(dots_out.at[which], dots_in.at[which, offset - 1], dots_send.at[which],
                   dots_recv.at[which], to["gx"], to["gy"]).start()

    def take_dots(which, number):
        whole = dots_in.at[which, pl.ds(0, count - 1)]
        pltpu.make_async_copy(whole, whole, dots_recv.at[which]).wait()
        row = jnp.sum(dots_in[which], axis=0)
        return [
            jnp.sum(jnp.where(tile_lane[:1] == index, row, 0.0), axis=1, keepdims=True)
            for index in range(number)
        ]

    @pl.loop(0, size_x, unroll=True)
    def _(i):
        put_field(0, field0, i, sens[i] / diagonal(i))

    zero = jnp.zeros((8, 128), jnp.float32)
    sent0 = start_exchange(0, field0)
    store_sens = pltpu.make_async_copy(sens, sens_out, store_sems.at[0])
    store_sens.start()
    finish_exchange(sent0)

    def first(i, sums):
        image = apply(0, field0, i)
        image0[i] = image
        put_field(1, field1, i, image / diagonal(i))
        scaled = field0[i + 1]
        return (sums[0] + fold(sens[i] * scaled), sums[1] + fold(image * scaled))

    dots = lax.fori_loop(0, size_x, first, (zero, zero), unroll=True)
    sent1 = start_exchange(1, field1)
    send_dots(0, dots)
    finish_exchange(sent1)

    @pl.loop(0, size_x, unroll=True)
    def _(i):
        image = apply(1, field1, i)
        image1[i] = image
        put_field(2, field2, i, image / diagonal(i))

    sent2 = start_exchange(2, field2)
    finish_exchange(sent2)

    @pl.loop(0, size_x, unroll=True)
    def _(i):
        image2[i] = apply(2, field2, i)

    g0, k0 = take_dots(0, 2)
    s0 = g0 / k0

    def second(i, sums):
        w1, im0, im1 = field1[i + 1], image0[i], image1[i]
        z1 = field0[i + 1] - s0 * w1
        r1 = sens[i] - s0 * im0
        az1 = im0 - s0 * im1
        y1 = w1 - s0 * field2[i + 1]
        ay1 = im1 - s0 * image2[i]
        terms = (r1 * z1, z1 * az1, y1 * az1, az1 * w1, w1 * im0, y1 * ay1, y1 * im1, w1 * im1)
        return tuple(total + fold(term) for total, term in zip(sums, terms))

    dots = lax.fori_loop(0, size_x, second, (zero,) * 8, unroll=True)
    send_dots(1, dots)
    g1, c1, d1, d2, d3, e1, e2, e3 = take_dots(1, 8)
    b1 = g1 / g0
    s1 = g1 / (c1 - b1 * g1 / s0)
    d0 = -g1 / s0
    g2 = g1 - 2.0 * s1 * (c1 + b1 * d0) + s1 * s1 * (d1 + 2.0 * b1 * d2 + b1 * b1 * d3)
    g2 = jnp.maximum(g2, 0.0)
    c2 = c1 - 2.0 * s1 * (d1 + b1 * d2) + s1 * s1 * (e1 + 2.0 * b1 * e2 + b1 * b1 * e3)
    b2 = g2 / g1
    s2 = g2 / (c2 - b2 * g2 / s1)
    t1 = s0 + s1 * (1.0 + b1)
    weight0 = t1 + s2 * (1.0 + b2 * (1.0 + b1))
    weight1 = -(s1 * s0 + s2 * (t1 + b2 * s0))
    weight2 = s2 * s0 * s1

    half = size_x // 2
    store_filt = []
    for part in range(2):
        span = pl.ds(part * half, half)
        for i in range(part * half, part * half + half):
            filt[i] = weight0 * field0[i + 1] + weight1 * field1[i + 1] + weight2 * field2[i + 1]
        store_filt.append(
            pltpu.make_async_copy(filt.at[span], filt_out.at[span], store_sems.at[1 + part])
        )
        store_filt[part].start()
    for copy, sends, _ in sent0 + sent1 + sent2:
        pl.when(sends)(copy.wait_send)
    for which in range(2):
        whole = dots_in.at[which, pl.ds(0, count - 1)]
        pltpu.make_async_copy(whole, whole, dots_send.at[which]).wait()
    store_sens.wait()
    for store in store_filt:
        store.wait()


def solution(mesh):
    n_x, n_y = mesh.shape["gx"], mesh.shape["gy"]

    def per_device(displacement, density, stiffness):
        size_x, size_y, size_z = density.shape
        block = (size_x, size_y, size_z)
        wide = pltpu.VMEM((size_x + 2, size_y, size_z), jnp.float32)
        same = pltpu.VMEM(block, jnp.float32)
        return pl.pallas_call(
            functools.partial(kernel, n_x, n_y),
            out_shape=(jax.ShapeDtypeStruct(block, jnp.float32),) * 2,
            in_specs=[pl.BlockSpec(memory_space=pltpu.HBM)] * 3,
            out_specs=(pl.BlockSpec(memory_space=pltpu.HBM),) * 2,
            scratch_shapes=[
                pltpu.VMEM(displacement.shape, jnp.float32),
                same,
                pltpu.SMEM(stiffness.shape, jnp.float32),
                pltpu.SemaphoreType.DMA((3,)),
                same,
                same,
                pltpu.SemaphoreType.DMA((3,)),
                pltpu.VMEM((4, 3, size_x + 1, size_y, size_z), jnp.float32),
                pltpu.VMEM((3, size_y, size_z), jnp.float32),
                pltpu.VMEM((3, size_x, size_z), jnp.float32),
                pltpu.VMEM((3, size_x, size_z), jnp.float32),
                pltpu.VMEM((8, size_z), jnp.float32),
                pltpu.VMEM((8, size_z), jnp.float32),
                wide, wide, wide, same, same, same,
                pltpu.VMEM((3, 2, size_x, size_z), jnp.float32),
                pltpu.VMEM((3, 2, size_x, size_z), jnp.float32),
                pltpu.VMEM((2, 1, 128), jnp.float32),
                pltpu.VMEM((2, n_x * n_y, 1, 128), jnp.float32),
                pltpu.SemaphoreType.DMA((3,)),
                pltpu.SemaphoreType.DMA((3,)),
                pltpu.SemaphoreType.DMA((3, 4)),
                pltpu.SemaphoreType.DMA((3, 4)),
                pltpu.SemaphoreType.DMA((2,)),
                pltpu.SemaphoreType.DMA((2,)),
            ],
            compiler_params=pltpu.CompilerParams(
                collective_id=0, has_side_effects=True, vmem_limit_bytes=62 * 1024 * 1024
            ),
        )(displacement, density, stiffness)

    return jax.shard_map(
        per_device,
        mesh=mesh,
        in_specs=(P(None, "gx", "gy", None), P("gx", "gy", None), P()),
        out_specs=(P("gx", "gy", None), P("gx", "gy", None)),
        check_vma=False,
    )
```

```python
import functools

import jax
import jax.numpy as jnp
from jax import lax
from jax.experimental import pallas as pl
from jax.experimental.pallas import tpu as pltpu
from jax.sharding import PartitionSpec as P

MESH = pl.DeviceIdType.MESH
penal = 3.0
e_min = 0.001
filter_weight = 2.0


def kernel(
    n_x, n_y,
    disp_in, dens_in, stiff_in,
    sens_out, filt_out,
    disp, dens, stiff, load_sems, sens, filt, store_sems,
    views, x_in, y_out, y_in, c_out, c_in,
    field0, field1, field2, image0, image1, image2, face_out, face_in, dots_out, dots_in,
    halo_send, halo_recv, face_send, face_recv, dots_send, dots_recv,
):
    size_x, size_y, size_z = dens.shape
    me_x, me_y = lax.axis_index("gx"), lax.axis_index("gy")
    me = me_x * n_y + me_y
    count = n_x * n_y
    has_xp, has_xn = me_x > 0, me_x < n_x - 1
    has_yp, has_yn = me_y > 0, me_y < n_y - 1

    def place(index):
        return {"gx": index // n_y, "gy": lax.rem(index, n_y)}

    loads = [
        pltpu.make_async_copy(disp_in, disp, load_sems.at[0]),
        pltpu.make_async_copy(stiff_in, stiff, load_sems.at[1]),
        pltpu.make_async_copy(dens_in, dens, load_sems.at[2]),
    ]
    for load in loads:
        load.start()
    barrier = pltpu.get_barrier_semaphore()

    @pl.loop(1, count, unroll=8)
    def _(offset):
        pl.semaphore_signal(
            barrier, inc=1, device_id=place(lax.rem(me + offset, count)), device_id_type=MESH
        )

    @pl.when(jnp.logical_not(has_xn))
    def _():
        x_in[...] = jnp.zeros_like(x_in)
        for field in (field0, field1, field2):
            field[size_x + 1] = jnp.zeros((size_y, size_z), jnp.float32)

    @pl.when(jnp.logical_not(has_xp))
    def _():
        for field in (field0, field1, field2):
            field[0] = jnp.zeros((size_y, size_z), jnp.float32)

    @pl.when(jnp.logical_not(has_yn))
    def _():
        y_in[...] = jnp.zeros_like(y_in)
        for step in range(3):
            face_in[step, 1] = jnp.zeros((size_x, size_z), jnp.float32)

    @pl.when(jnp.logical_not(has_yp))
    def _():
        for step in range(3):
            face_in[step, 0] = jnp.zeros((size_x, size_z), jnp.float32)

    @pl.when(jnp.logical_not(jnp.logical_and(has_xn, has_yn)))
    def _():
        c_in[...] = jnp.zeros_like(c_in)

    loads[0].wait()
    pl.semaphore_wait(barrier, count - 1)

    def remote(src, dst, send, recv, to_x, to_y):
        return pltpu.make_async_remote_copy(
            src_ref=src, dst_ref=dst, send_sem=send, recv_sem=recv,
            device_id={"gx": to_x, "gy": to_y}, device_id_type=MESH,
        )

    halo_x = remote(disp.at[:, 0], x_in, halo_send.at[0], halo_recv.at[0], me_x - 1, me_y)
    halo_y = remote(y_out, y_in, halo_send.at[1], halo_recv.at[1], me_x, me_y - 1)
    halo_c = remote(c_out, c_in, halo_send.at[2], halo_recv.at[2], me_x - 1, me_y - 1)
    halos = (
        (halo_x, has_xp, has_xn),
        (halo_y, has_yp, has_yn),
        (halo_c, jnp.logical_and(has_xp, has_yp), jnp.logical_and(has_xn, has_yn)),
    )
    pl.when(has_xp)(halo_x.start)
    c_out[...] = jnp.zeros_like(c_out)
    for m in range(3):
        for i in range(size_x):
            y_out[m, i : i + 1, :] = disp[m, i, 0:1, :]
        c_out[m : m + 1, :] = disp[m, 0, 0:1, :]

    for copy, sends, _ in halos[1:]:
        pl.when(sends)(copy.start)

    rows = lax.broadcasted_iota(jnp.int32, (size_y, size_z), 0)
    lanes = lax.broadcasted_iota(jnp.int32, (size_y, size_z), 1)

    def later_z(value):
        return jnp.where(lanes == size_z - 1, 0.0, pltpu.roll(value, size_z - 1, 1))

    def earlier_z(value):
        return jnp.where(lanes == 0, 0.0, pltpu.roll(value, 1, 1))

    def put_views(m, i, value, last_row):
        upper = pltpu.roll(value, size_y - 1, 0)
        if last_row is not None:
            upper = jnp.where(rows == size_y - 1, jnp.broadcast_to(last_row, value.shape), upper)
        views[0, m, i] = value
        views[1, m, i] = later_z(value)
        views[2, m, i] = upper
        views[3, m, i] = later_z(upper)

    @pl.loop(0, size_x, unroll=True)
    def _(i):
        for m in range(3):
            put_views(m, i, disp[m, i], None)

    def energy_block(i, start):
        def view(dof):
            a, b, c, m = dof // 12, dof // 6 % 2, dof // 3 % 2, dof % 3
            return views[2 * b + c, m, i + a, start : start + 8, :]

        energy = None
        for row in range(24):
            weighted = (0.5 * stiff[row, row]) * view(row)
            for col in range(row + 1, 24):
                weighted = weighted + stiff[row, col] * view(col)
            term = view(row) * weighted
            energy = term if energy is None else energy + term
        rho = dens[i, start : start + 8, :]
        sens[i, start : start + 8, :] = (-2.0 * penal * (1.0 - e_min)) * (rho * rho) * energy

    loads[1].wait()
    loads[2].wait()

    @pl.loop(0, size_x - 1)
    def _(i):
        energy_block(i, 0)

    for copy, sends, receives in halos:
        pl.when(receives)(copy.wait_recv)
    for m in range(3):
        put_views(m, size_x, x_in[m], c_in[m : m + 1, :])

    @pl.loop(0, size_x, unroll=True)
    def _(i):
        for m in range(3):
            last = y_in[m, pl.ds(i, 1), :]
            views[2, m, i, size_y - 1 : size_y, :] = last
            views[3, m, i, size_y - 1 : size_y, :] = jnp.where(
                lanes[:1] == size_z - 1, 0.0, pltpu.roll(last, size_z - 1, 1)
            )

    for start in range(8, size_y, 8):
        @pl.loop(0, size_x)
        def _(i):
            energy_block(i, start)

    energy_block(size_x - 1, 0)

    for copy, sends, _ in halos:
        pl.when(sends)(copy.wait_send)

    plane = 6.0 - (lanes == 0).astype(jnp.float32) - (lanes == size_z - 1).astype(jnp.float32)
    row_low = jnp.logical_and(rows == 0, jnp.logical_not(has_yp))
    row_high = jnp.logical_and(rows == size_y - 1, jnp.logical_not(has_yn))
    plane = plane - row_low.astype(jnp.float32) - row_high.astype(jnp.float32)

    def diagonal(i):
        at_low = jnp.logical_and(i == 0, jnp.logical_not(has_xp))
        at_high = jnp.logical_and(i == size_x - 1, jnp.logical_not(has_xn))
        missing = at_low.astype(jnp.float32) + at_high.astype(jnp.float32)
        return 1.0 + filter_weight * (plane - missing)

    def put_field(step, field, i, value):
        field[i + 1] = value
        face_out[step, 0, pl.ds(i, 1), :] = value[0:1]
        face_out[step, 1, pl.ds(i, 1), :] = value[size_y - 1 : size_y]

    def faces(step, field):
        return (
            (remote(field.at[1], field.at[size_x + 1], face_send.at[step, 0],
                    face_recv.at[step, 0], me_x - 1, me_y), has_xp, has_xn),
            (remote(field.at[size_x], field.at[0], face_send.at[step, 1],
                    face_recv.at[step, 1], me_x + 1, me_y), has_xn, has_xp),
            (remote(face_out.at[step, 0], face_in.at[step, 1], face_send.at[step, 2],
                    face_recv.at[step, 2], me_x, me_y - 1), has_yp, has_yn),
            (remote(face_out.at[step, 1], face_in.at[step, 0], face_send.at[step, 3],
                    face_recv.at[step, 3], me_x, me_y + 1), has_yn, has_yp),
        )

    def start_exchange(step, field):
        copies = faces(step, field)
        for copy, sends, _ in copies:
            pl.when(sends)(copy.start)
        return copies

    def finish_exchange(copies):
        for copy, _, receives in copies:
            pl.when(receives)(copy.wait_recv)

    def apply(step, field, i):
        value = field[i + 1]
        below = jnp.where(rows == 0, jnp.broadcast_to(face_in[step, 0, pl.ds(i, 1), :], value.shape),
                          pltpu.roll(value, 1, 0))
        above = jnp.where(rows == size_y - 1,
                          jnp.broadcast_to(face_in[step, 1, pl.ds(i, 1), :], value.shape),
                          pltpu.roll(value, size_y - 1, 0))
        beside = field[i] + field[i + 2] + below + above + later_z(value) + earlier_z(value)
        return diagonal(i) * value - filter_weight * beside

    def fold(value):
        part = value[0:8]
        for start in range(8, size_y, 8):
            part = part + value[start : start + 8]
        total = part[:, 0:128]
        for start in range(128, size_z, 128):
            total = total + part[:, start : start + 128]
        return total

    tile_row = lax.broadcasted_iota(jnp.int32, (8, 128), 0)
    tile_lane = lax.broadcasted_iota(jnp.int32, (8, 128), 1)

    def send_dots(which, parts):
        packed = jnp.zeros((8, 128), jnp.float32)
        for index, part in enumerate(parts):
            packed = packed + jnp.where(
                tile_row == index, jnp.broadcast_to(jnp.sum(part, axis=0, keepdims=True), (8, 128)), 0.0
            )
        totals = jnp.broadcast_to(jnp.sum(packed, axis=1, keepdims=True), (8, 128))
        row = jnp.sum(jnp.where(tile_row == tile_lane, totals, 0.0), axis=0, keepdims=True)
        dots_out[which] = row
        dots_in[which, count - 1] = row

        @pl.loop(1, count, unroll=8)
        def _(offset):
            to = place(lax.rem(me + offset, count))
            remote(dots_out.at[which], dots_in.at[which, offset - 1], dots_send.at[which],
                   dots_recv.at[which], to["gx"], to["gy"]).start()

    def take_dots(which, number):
        whole = dots_in.at[which, pl.ds(0, count - 1)]
        pltpu.make_async_copy(whole, whole, dots_recv.at[which]).wait()
        row = jnp.sum(dots_in[which], axis=0)
        return [
            jnp.sum(jnp.where(tile_lane[:1] == index, row, 0.0), axis=1, keepdims=True)
            for index in range(number)
        ]

    @pl.loop(0, size_x, unroll=True)
    def _(i):
        put_field(0, field0, i, sens[i] / diagonal(i))

    zero = jnp.zeros((8, 128), jnp.float32)
    sent0 = start_exchange(0, field0)
    store_sens = pltpu.make_async_copy(sens, sens_out, store_sems.at[0])
    store_sens.start()
    finish_exchange(sent0)

    def first(i, sums):
        image = apply(0, field0, i)
        image0[i] = image
        put_field(1, field1, i, image / diagonal(i))
        scaled = field0[i + 1]
        return (sums[0] + fold(sens[i] * scaled), sums[1] + fold(image * scaled))

    dots = lax.fori_loop(0, size_x, first, (zero, zero), unroll=True)
    sent1 = start_exchange(1, field1)
    send_dots(0, dots)
    finish_exchange(sent1)

    @pl.loop(0, size_x, unroll=True)
    def _(i):
        image = apply(1, field1, i)
        image1[i] = image
        put_field(2, field2, i, image / diagonal(i))

    sent2 = start_exchange(2, field2)
    finish_exchange(sent2)

    @pl.loop(0, size_x, unroll=True)
    def _(i):
        image2[i] = apply(2, field2, i)

    g0, k0 = take_dots(0, 2)
    s0 = g0 / k0

    def second(i, sums):
        w1, im0, im1 = field1[i + 1], image0[i], image1[i]
        z1 = field0[i + 1] - s0 * w1
        r1 = sens[i] - s0 * im0
        az1 = im0 - s0 * im1
        y1 = w1 - s0 * field2[i + 1]
        ay1 = im1 - s0 * image2[i]
        terms = (r1 * z1, z1 * az1, y1 * az1, az1 * w1, w1 * im0, y1 * ay1, y1 * im1, w1 * im1)
        return tuple(total + fold(term) for total, term in zip(sums, terms))

    dots = lax.fori_loop(0, size_x, second, (zero,) * 8, unroll=True)
    send_dots(1, dots)
    g1, c1, d1, d2, d3, e1, e2, e3 = take_dots(1, 8)
    b1 = g1 / g0
    s1 = g1 / (c1 - b1 * g1 / s0)
    d0 = -g1 / s0
    g2 = g1 - 2.0 * s1 * (c1 + b1 * d0) + s1 * s1 * (d1 + 2.0 * b1 * d2 + b1 * b1 * d3)
    g2 = jnp.maximum(g2, 0.0)
    c2 = c1 - 2.0 * s1 * (d1 + b1 * d2) + s1 * s1 * (e1 + 2.0 * b1 * e2 + b1 * b1 * e3)
    b2 = g2 / g1
    s2 = g2 / (c2 - b2 * g2 / s1)
    t1 = s0 + s1 * (1.0 + b1)
    weight0 = t1 + s2 * (1.0 + b2 * (1.0 + b1))
    weight1 = -(s1 * s0 + s2 * (t1 + b2 * s0))
    weight2 = s2 * s0 * s1

    half = size_x // 2
    store_filt = []
    for part in range(2):
        span = pl.ds(part * half, half)
        for i in range(part * half, part * half + half):
            filt[i] = weight0 * field0[i + 1] + weight1 * field1[i + 1] + weight2 * field2[i + 1]
        store_filt.append(
            pltpu.make_async_copy(filt.at[span], filt_out.at[span], store_sems.at[1 + part])
        )
        store_filt[part].start()
    for copy, sends, _ in sent0 + sent1 + sent2:
        pl.when(sends)(copy.wait_send)
    for which in range(2):
        whole = dots_in.at[which, pl.ds(0, count - 1)]
        pltpu.make_async_copy(whole, whole, dots_send.at[which]).wait()
    store_sens.wait()
    for store in store_filt:
        store.wait()


def solution(mesh):
    n_x, n_y = mesh.shape["gx"], mesh.shape["gy"]

    def per_device(displacement, density, stiffness):
        size_x, size_y, size_z = density.shape
        block = (size_x, size_y, size_z)
        wide = pltpu.VMEM((size_x + 2, size_y, size_z), jnp.float32)
        same = pltpu.VMEM(block, jnp.float32)
        return pl.pallas_call(
            functools.partial(kernel, n_x, n_y),
            out_shape=(jax.ShapeDtypeStruct(block, jnp.float32),) * 2,
            in_specs=[pl.BlockSpec(memory_space=pltpu.HBM)] * 3,
            out_specs=(pl.BlockSpec(memory_space=pltpu.HBM),) * 2,
            scratch_shapes=[
                pltpu.VMEM(displacement.shape, jnp.float32),
                same,
                pltpu.SMEM(stiffness.shape, jnp.float32),
                pltpu.SemaphoreType.DMA((3,)),
                same,
                same,
                pltpu.SemaphoreType.DMA((3,)),
                pltpu.VMEM((4, 3, size_x + 1, size_y, size_z), jnp.float32),
                pltpu.VMEM((3, size_y, size_z), jnp.float32),
                pltpu.VMEM((3, size_x, size_z), jnp.float32),
                pltpu.VMEM((3, size_x, size_z), jnp.float32),
                pltpu.VMEM((8, size_z), jnp.float32),
                pltpu.VMEM((8, size_z), jnp.float32),
                wide, wide, wide, same, same, same,
                pltpu.VMEM((3, 2, size_x, size_z), jnp.float32),
                pltpu.VMEM((3, 2, size_x, size_z), jnp.float32),
                pltpu.VMEM((2, 1, 128), jnp.float32),
                pltpu.VMEM((2, n_x * n_y, 1, 128), jnp.float32),
                pltpu.SemaphoreType.DMA((3,)),
                pltpu.SemaphoreType.DMA((3,)),
                pltpu.SemaphoreType.DMA((3, 4)),
                pltpu.SemaphoreType.DMA((3, 4)),
                pltpu.SemaphoreType.DMA((2,)),
                pltpu.SemaphoreType.DMA((2,)),
            ],
            compiler_params=pltpu.CompilerParams(
                collective_id=0, has_side_effects=True, vmem_limit_bytes=62 * 1024 * 1024
            ),
        )(displacement, density, stiffness)

    return jax.shard_map(
        per_device,
        mesh=mesh,
        in_specs=(P(None, "gx", "gy", None), P("gx", "gy", None), P()),
        out_specs=(P("gx", "gy", None), P("gx", "gy", None)),
        check_vma=False,
    )
```
